32 devices in a mesh: dp: 8 (over z, x), fsdp: 4 (over y, core).
Axes of the slice: x: 2, y: 2, z: 4, core: 2. Of those that a mesh axis runs over, the one named last changes fastest.
Arguments:
- query_tokens: bfloat16 [128, 128, 768], P(('dp', 'fsdp')), may hold values from -6 to 6
- passage_tokens: bfloat16 [32, 512, 768], P(('dp', 'fsdp')), may hold values from -6 to 6
- query_lengths: int32 [128], P(('dp', 'fsdp')), may hold values from 0 to 128, as said below
- passage_lengths: int32 [32], P(('dp', 'fsdp')), may hold values from 0 to 512, as said below
- query_cotangent: bfloat16 [128, 128, 768], P(('dp', 'fsdp')), may hold values from -6 to 6
- passage_cotangent: bfloat16 [32, 512, 768], P(('dp', 'fsdp')), may hold values from -6 to 6
- qkv_weight: bfloat16 [768, 2304], P(('dp', 'fsdp')), may hold values from -0.21875 to 0.21875
- out_weight: bfloat16 [768, 768], P(('dp', 'fsdp')), may hold values from -1.75 to 1.75
- inner_weight: bfloat16 [768, 3072], P(('dp', 'fsdp')), may hold values from -0.21875 to 0.21875
- outer_weight: bfloat16 [3072, 768], P(('dp', 'fsdp')), may hold values from -0.109375 to 0.109375
- ln_gains: bfloat16 [2, 768], P(None, ('dp', 'fsdp')), may hold values from 0.5 to 1.5
- bias_rows: bfloat16 [6, 768], P(None, ('dp', 'fsdp')), may hold values from -3 to 3
- inner_bias: bfloat16 [3072], P(('dp', 'fsdp')), may hold values from -3 to 3
Outputs:
- query_out: bfloat16 [128, 128, 768], P(('dp', 'fsdp'))
- passage_out: bfloat16 [32, 512, 768], P(('dp', 'fsdp'))
- query_grad: bfloat16 [128, 128, 768], P(('dp', 'fsdp'))
- passage_grad: bfloat16 [32, 512, 768], P(('dp', 'fsdp'))
- grad_qkv: float32 [768, 2304], P(('dp', 'fsdp'))
- grad_out: float32 [768, 768], P(('dp', 'fsdp'))
- grad_inner: float32 [768, 3072], P(('dp', 'fsdp'))
- grad_outer: float32 [3072, 768], P(('dp', 'fsdp'))
- grad_gains: float32 [2, 768], P(None, ('dp', 'fsdp'))
- grad_biases: float32 [6, 768], P(None, ('dp', 'fsdp'))
- grad_inner_bias: float32 [3072], P(('dp', 'fsdp'))
The draws below stay inside these ranges and needn't reach their ends.
Inputs may be any that keep to these rules, and one draw needn't show every extreme that they name: `query_lengths`: on each device the used slots of its 4 query slots come first; every device uses at least 2, some device all of them. A used slot holds 64 to 128 real tokens, an unused one 0; some sequence has exactly 128. `passage_lengths`: on each device the used slots of its 1 passage slots come first; every device uses at least 0, some device all of them. A used slot holds 256 to 512 real tokens, an unused one 0; some sequence has exactly 512.
All inputs are finite; a program needn't handle non-finite values.
Results may differ from the reference program's by a relative error of at most 0.014.
Values may be sent and summed in bfloat16 or wider, within the bound.
No kernel may reach another device: no remote copies, remote signals or barrier semaphores. Data moves between devices by JAX's collectives and lax.ppermute only.
A program may use at most 192 MiB of HBM per device.

```python
import math
import jax
import jax.numpy as jnp
from jax import lax

D = 768
HEADS = 12
HEAD = 64
FF = 3072
QLEN = 128
PLEN = 512
QS_DEV = 4
PS_DEV = 1
NQS = 128
NPS = 32


def slot_lengths(key, slots, per_device, longest):
    devices_count = slots // per_device
    count_key, full_key, length_key = jax.random.split(key, 3)
    counts = jax.random.randint(count_key, (devices_count,), per_device // 2, per_device + 1)
    full_device = jax.random.randint(full_key, (), 0, devices_count)
    counts = jnp.where(jnp.arange(devices_count) == full_device, per_device, counts)
    used_slots = (jnp.arange(per_device)[None, :] < counts[:, None]).reshape(-1)
    lengths = jax.random.randint(length_key, (slots,), longest // 2, longest + 1)
    lengths = jnp.where(jnp.arange(slots) == full_device * per_device, longest, lengths)
    return jnp.where(used_slots, lengths, 0).astype(jnp.int32)


def draw_query_lengths(key, part):
    return slot_lengths(jax.random.fold_in(key, 11), NQS, QS_DEV, QLEN)


def draw_passage_lengths(key, part):
    return slot_lengths(jax.random.fold_in(key, 29), NPS, PS_DEV, PLEN)


def shard_levels(own_key, extent, cuts, least, largest):
    loudness = 1.0
    for position, shards_of in cuts:
        steps = jax.random.uniform(jax.random.fold_in(jax.random.fold_in(own_key, 6), position), (shards_of,), jnp.float32, least / len(cuts), largest / len(cuts))
        loudness = loudness * jnp.repeat(jnp.exp(steps), extent[position] // shards_of).reshape((-1,) + (1,) * (len(extent) - 1 - position))
    return loudness


def gaussian(rng, extent, width, reach, shards=(), held_as=jnp.bfloat16):
    drawn = jax.random.normal(rng, extent, jnp.float32) * width
    if len(shards) > 0:
        drawn = shard_levels(rng, extent, shards, -0.22, 0.18) * drawn
    return jnp.clip(drawn, min=-reach, max=reach).astype(held_as)


def setup_inputs(seed: int = 0) -> dict:
    splits = jax.random.split(jax.random.key(seed), 14)
    return {
        "query_tokens": gaussian(splits[0], (NQS, QLEN, D), 1.0, 6.0, ((0, 32),)),
        "passage_tokens": gaussian(splits[1], (NPS, PLEN, D), 1.0, 6.0, ((0, 32),)),
        "query_lengths": draw_query_lengths(jax.random.fold_in(splits[13], 71), 0),
        "passage_lengths": draw_passage_lengths(jax.random.fold_in(splits[13], 71), 0),
        "query_cotangent": gaussian(splits[4], (NQS, QLEN, D), 1.0, 6.0, ((0, 32),)),
        "passage_cotangent": gaussian(splits[5], (NPS, PLEN, D), 1.0, 6.0, ((0, 32),)),
        "qkv_weight": gaussian(splits[6], (D, 3 * D), D ** -0.5, 0.21875, ((0, 32),)),
        "out_weight": gaussian(splits[7], (D, D), (D // 64) ** -0.5, 1.75, ((0, 32),)),
        "inner_weight": gaussian(splits[8], (D, FF), D ** -0.5, 0.21875, ((0, 32),)),
        "outer_weight": gaussian(splits[9], (FF, D), FF ** -0.5, 0.109375, ((0, 32),)),
        "ln_gains": jnp.clip(1.0 + 0.1 * jax.random.normal(splits[10], (2, D), jnp.float32), 0.5, 1.5).astype(jnp.bfloat16),
        "bias_rows": gaussian(splits[11], (6, D), 0.5, 3.0, ((1, 32),)),
        "inner_bias": gaussian(splits[12], (FF,), 0.5, 3.0, ((0, 32),)),
    }


@jax.custom_vjp
def low(v):
    return lax.optimization_barrier(v.astype(jnp.bfloat16)).astype(jnp.float32)

@jax.custom_vjp
def low_back(v):
    return v

def low_keep(v):
    return (low(v), None)

def low_pass(kept, grad):
    return (grad,)

def back_keep(v):
    return (v, None)

def back_low(kept, grad):
    return (low(grad),)
low.defvjp(low_keep, low_pass)
low_back.defvjp(back_keep, back_low)
EPSILON = 1e-12
PRECISE = lax.Precision.HIGHEST

def layer_norm(hidden, gain_vec, shift_vec):
    center = hidden - lax.optimization_barrier(jnp.mean(hidden, axis=-1, keepdims=True))
    spread = lax.optimization_barrier(jnp.mean(center * center, axis=-1, keepdims=True))
    return center * lax.rsqrt(spread + EPSILON) * gain_vec + shift_vec

def layer(params, inputs, lengths):
    qkv_weight, out_weight, inner_weight, outer_weight, ln_gains, bias_rows, inner_bias = params
    seq_count, seq_length, model_width = inputs.shape
    valid_rows = jnp.arange(seq_length)[None, :] < lengths[:, None]
    qkv_shift = jnp.concatenate([bias_rows[0], jnp.zeros((model_width,), jnp.float32), bias_rows[1]])
    projected = jnp.einsum('bld,de->ble', inputs, qkv_weight, precision=PRECISE)
    qkv_all = low(low_back(projected) + qkv_shift)
    heads_view = qkv_all.reshape(seq_count, seq_length, 3, HEADS, HEAD)
    queries = heads_view[:, :, 0]
    keys_all = heads_view[:, :, 1]
    values = heads_view[:, :, 2]
    scores = jnp.einsum('blhe,bmhe->bhlm', queries, keys_all, precision=PRECISE) * 0.125
    scores = low_back(jnp.where(valid_rows[:, None, None, :], scores, -1000000000.0))
    weights = low(jax.nn.softmax(scores, axis=-1))
    context = jnp.einsum('bhlm,bmhe->blhe', weights, values, precision=PRECISE)
    context = low(low_back(context.reshape(seq_count, seq_length, model_width)))
    attended = low_back(jnp.einsum('bld,de->ble', context, out_weight, precision=PRECISE)) + bias_rows[2]
    normed = layer_norm(inputs + attended, ln_gains[0], bias_rows[3])
    upward = low_back(jnp.einsum('bld,df->blf', low(normed), inner_weight, precision=PRECISE)) + inner_bias
    activated = low(jax.nn.gelu(upward, approximate=False))
    downward = low_back(jnp.einsum('blf,fd->bld', activated, outer_weight, precision=PRECISE)) + bias_rows[4]
    result = layer_norm(normed + downward, ln_gains[1], bias_rows[5])
    return jnp.where(valid_rows[:, :, None], result, 0.0)

def bucket_pass(params, tokens, cotangent, lengths, group):
    total = tokens.shape[0]
    steps_count = total // group
    tok_groups = tokens.reshape((steps_count, group) + tokens.shape[1:])
    cot_groups = cotangent.reshape((steps_count, group) + tokens.shape[1:])
    len_groups = lengths.reshape(steps_count, group)

    def one_group(carry, item):
        tok_group, cot_group, len_group = item

        def local(param_set, values_in):
            return layer(param_set, values_in, len_group)
        output, backward = jax.vjp(local, params, tok_group.astype(jnp.float32))
        param_grad, input_grad = backward(cot_group.astype(jnp.float32))
        carry = jax.tree.map(lambda left, right: left + right, carry, param_grad)
        return (carry, (output.astype(jnp.bfloat16), input_grad.astype(jnp.bfloat16)))
    start = jax.tree.map(jnp.zeros_like, params)
    grads, (outputs, input_grads) = lax.scan(one_group, start, (tok_groups, cot_groups, len_groups))
    return (grads, outputs.reshape(tokens.shape), input_grads.reshape(tokens.shape))

def reference(query_tokens, passage_tokens, query_lengths, passage_lengths, query_cotangent, passage_cotangent, qkv_weight, out_weight, inner_weight, outer_weight, ln_gains, bias_rows, inner_bias):
    params = tuple((item.astype(jnp.float32) for item in (qkv_weight, out_weight, inner_weight, outer_weight, ln_gains, bias_rows, inner_bias)))
    query_group = math.gcd(NQS, max(1, 4096 // QLEN))
    passage_group = math.gcd(NPS, max(1, 4096 // PLEN))
    query_grads, query_out, query_grad = bucket_pass(params, query_tokens, query_cotangent, query_lengths, query_group)
    passage_grads, passage_out, passage_grad = bucket_pass(params, passage_tokens, passage_cotangent, passage_lengths, passage_group)
    totals = jax.tree.map(lambda left, right: left + right, query_grads, passage_grads)
    return (query_out, passage_out, query_grad, passage_grad, totals[0], totals[1], totals[2], totals[3], totals[4], totals[5], totals[6])
```

```python
import functools
import math

import jax
import jax.numpy as jnp
from jax import lax
from jax.experimental import pallas as pl
from jax.experimental.pallas import tpu as pltpu
from jax.sharding import PartitionSpec as P

HEADS = 12
EPSILON = 1e-12
MASKED = -1000000000.0
LOG2E = math.log2(math.e)
AXES = ("dp", "fsdp")
BF = jnp.bfloat16
F32 = jnp.float32
TAIL_P = 0.34
TAIL_C = (
    0.1357184499502182,
    0.13244222104549408,
    0.14697369933128357,
    -0.012965014204382896,
    0.246027871966362,
    -0.1909387707710266,
    0.04274154454469681,
)
VM = pl.BlockSpec(memory_space=pltpu.VMEM)
SM = pl.BlockSpec(memory_space=pltpu.SMEM)


def sds(shape, dtype):
    return jax.ShapeDtypeStruct(shape, dtype)


def params(mib):
    return pltpu.CompilerParams(vmem_limit_bytes=int(mib * 2**20))


def cost(flops=0, nbytes=0, trans=0):
    return pl.CostEstimate(flops=int(flops), bytes_accessed=int(nbytes), transcendentals=int(trans))


def mm(a, b):
    return lax.dot_general(a, b, (((1,), (0,)), ((), ())), preferred_element_type=F32)


def mm_nt(a, b):
    return lax.dot_general(a, b, (((1,), (1,)), ((), ())), preferred_element_type=F32)


def mm_tn(a, b):
    return lax.dot_general(a, b, (((0,), (0,)), ((), ())), preferred_element_type=F32)


class Net:
    def __init__(self, mesh):
        self.inner = mesh.shape["fsdp"]
        self.n = mesh.shape["dp"] * self.inner
        bits = self.n.bit_length() - 1
        self.core = [0, 1]
        self.xy = [0, 2, 4, 6]
        self.far = [k << 3 for k in range(self.n >> 3)]
        self.usable = self.n == 1 << bits and bits >= 4

    def index(self):
        return lax.axis_index("dp") * self.inner + lax.axis_index("fsdp")

    def swap(self, x, k):
        return lax.ppermute(x, AXES, [(i, i ^ k) for i in range(self.n)])

    def stack(self, pieces):
        k, r, c = pieces[0].shape
        m = len(pieces)

        def body(*refs):
            for i in range(m):
                refs[-1][i * k : (i + 1) * k] = refs[i][...]

        size = m * pieces[0].size * 2
        return pl.pallas_call(
            body,
            out_shape=sds((m * k, r, c), pieces[0].dtype),
            in_specs=[VM] * m,
            out_specs=VM,
            compiler_params=params(2 * size / 2**20 + 1),
            cost_estimate=cost(0, size),
        )(*pieces)

    def gather_pieces(self, block):
        far = self.stack([block] + [self.swap(block, k) for k in self.far[1:]])
        near = self.stack([far] + [self.swap(far, k) for k in self.xy[1:]])
        offs = [x ^ z for x in self.xy for z in self.far]
        return [(near, offs), (self.swap(near, 1), [o ^ 1 for o in offs])]


def place(net, pieces, parts):
    total = len(pieces)

    def body(*refs):
        idx = net.index()
        outs = refs[total:]
        for ref, (_, offs) in zip(refs, pieces):
            for j, off in enumerate(offs):
                owner = idx ^ off
                for out, (col, rows, groups, width) in zip(outs, parts):
                    for g in range(groups):
                        out[owner, g * rows : (g + 1) * rows, :] = ref[
                            j, :rows, col + g * width : col + (g + 1) * width
                        ]

    size = sum(a.size * 2 for a, _ in pieces)
    return pl.pallas_call(
        body,
        out_shape=[sds((net.n, rows * groups, width), BF) for _, rows, groups, width in parts],
        in_specs=[VM] * total,
        out_specs=[VM] * len(parts),
        compiler_params=params(2 * size / 2**20 + 1),
        cost_estimate=cost(0, size),
    )(*[a for a, _ in pieces])


def scatter_sum(net, grad):
    n, r, c = grad.shape
    offs = [x ^ z for x in net.xy for z in net.far]
    nz = len(net.far)
    idx_of = net.index

    def first(g, out):
        idx = idx_of()
        for j, off in enumerate(offs):
            out[j] = g[idx ^ off ^ 1].astype(BF)

    half = len(offs) * r * c
    send = pl.pallas_call(
        first,
        out_shape=sds((len(offs), r, c), BF),
        in_specs=[VM],
        out_specs=VM,
        compiler_params=params((half * 12 + half * 0) / 2**20 + 1),
        cost_estimate=cost(0, half * 6),
    )(grad)
    got = net.swap(send, 1)

    def second(g, a, *outs):
        idx = idx_of()
        for o, out in enumerate(outs):
            for z in range(nz):
                j = (o + 1) * nz + z
                out[z] = (g[idx ^ offs[j]] + a[j].astype(F32)).astype(BF)

    sends = pl.pallas_call(
        second,
        out_shape=[sds((nz, r, c), BF)] * 3,
        in_specs=[VM, VM],
        out_specs=[VM] * 3,
        compiler_params=params(half * 14 / 2**20 + 1),
        cost_estimate=cost(0, half * 6),
    )(grad, got)
    got2 = [net.swap(s, k) for s, k in zip(sends, net.xy[1:])]

    def third(g, a, b0, b1, b2, own, *outs):
        idx = idx_of()
        for z in range(nz):
            t = g[idx ^ offs[z]] + a[z].astype(F32)
            t = t + b0[z].astype(F32) + b1[z].astype(F32) + b2[z].astype(F32)
            if z == 0:
                own[...] = t
            else:
                outs[z - 1][0] = t.astype(BF)

    res = pl.pallas_call(
        third,
        out_shape=[sds((r, c), F32)] + [sds((1, r, c), BF)] * (nz - 1),
        in_specs=[VM] * 5,
        out_specs=[VM] * nz,
        compiler_params=params(half * 14 / 2**20 + 1),
        cost_estimate=cost(0, half * 3),
    )(grad, got, *got2)
    total = res[0]
    for s, k in zip(res[1:], net.far[1:]):
        total = total + net.swap(s, k)[0].astype(F32)
    return total


class Shape:
    def __init__(self, queries, qlen, passages, plen):
        self.rq = queries * qlen
        self.rp = passages * plen
        self.rows = self.rq + self.rp
        self.segs = [(i * qlen, qlen, 0, i) for i in range(queries)]
        self.segs += [(self.rq + i * plen, plen, 1, i) for i in range(passages)]
        self.block = math.gcd(256, math.gcd(self.rq, self.rp))
        self.steps = self.rows // self.block
        self.nq = self.rq // self.block

    def valid(self, i, lens):
        row = lax.broadcasted_iota(jnp.int32, (self.block, 1), 0) + i * self.block
        ok = None
        for base, _, which, k in self.segs:
            here = (row >= base) & (row < base + lens[which][k])
            ok = here if ok is None else ok | here
        return ok

    def both(self, width):
        b, nq = self.block, self.nq
        return [
            pl.BlockSpec((b, width), lambda i, *_: (jnp.minimum(i, nq - 1), 0)),
            pl.BlockSpec((b, width), lambda i, *_: (jnp.maximum(i - nq, 0), 0)),
        ]

    def rowspec(self, width):
        return pl.BlockSpec((self.block, width), lambda i, *_: (i, 0))


def once(shape):
    return pl.BlockSpec(shape, lambda i, *_: (0,) * len(shape))


def qkv_project(sh, xq, xp, w, shift):
    d = xq.shape[1]
    width = shift.shape[1]

    def body(xq, xp, w, b, o):
        i = pl.program_id(0)
        x = jnp.where(i < sh.nq, xq[...], xp[...])
        for c in range(0, width, d):
            o[:, c : c + d] = (mm(x, w[:, c : c + d]) + b[:, c : c + d]).astype(BF)

    return pl.pallas_call(
        body,
        grid=(sh.steps,),
        out_shape=sds((sh.rows, width), BF),
        in_specs=sh.both(d) + [VM, VM],
        out_specs=sh.rowspec(width),
        compiler_params=params(24),
        cost_estimate=cost(2 * sh.rows * d * width, sh.rows * (d + width) * 2),
    )(xq, xp, w, shift)


def attend(sh, lens, qkv):
    d = qkv.shape[1] // 3
    hd = d // HEADS
    pw = 2 * hd
    pairs = HEADS // 2

    def body(ql, pln, q, k, v, ctx, lse):
        lane = lax.broadcasted_iota(jnp.int32, (1, pw), 1)
        for base, ln, which, i in sh.segs:
            n = (ql, pln)[which][i]
            rows = slice(base, base + ln)
            qb, kb, vb = q[rows, :], k[rows, :], v[rows, :]
            vt = vb.T
            keep = lax.broadcasted_iota(jnp.int32, (ln, 1), 0) < n
            outs = []
            for h in range(2):
                kh = jnp.where((lane >= h * hd) & (lane < (h + 1) * hd), kb, jnp.zeros_like(kb))
                s = mm_nt(kh, qb) * (0.125 * LOG2E)
                s = jnp.where(keep, s, MASKED * LOG2E)
                top = jnp.max(s, axis=0, keepdims=True)
                e = jnp.exp2(s - top)
                tot = jnp.sum(e, axis=0, keepdims=True)
                outs.append(mm(vt[h * hd : (h + 1) * hd], e.astype(BF)) * (1.0 / tot))
                lse[0, h : h + 1, rows] = top + jnp.log(tot) * LOG2E
            ctx[rows, :] = jnp.concatenate(outs, axis=0).T.astype(BF)

    def col(c):
        return pl.BlockSpec((sh.rows, pw), lambda j, *_: (0, c * pairs + j))

    grid_spec = pltpu.PrefetchScalarGridSpec(
        num_scalar_prefetch=2,
        grid=(pairs,),
        in_specs=[col(0), col(1), col(2)],
        out_specs=[col(0), pl.BlockSpec((1, 2, sh.rows), lambda j, *_: (j, 0, 0))],
    )
    sq = sum(ln * ln for _, ln, _, _ in sh.segs)
    return pl.pallas_call(
        body,
        grid_spec=grid_spec,
        out_shape=[sds((sh.rows, d), BF), sds((pairs, 2, sh.rows), F32)],
        compiler_params=params(24),
        cost_estimate=cost(4 * 4 * sq * d, sh.rows * d * 8, sq * HEADS),
    )(*lens, qkv, qkv, qkv)


def attend_back(sh, lens, qkv, ctx, dctx, lse):
    d = qkv.shape[1] // 3
    hd = d // HEADS
    pw = 2 * hd
    pairs = HEADS // 2

    def body(ql, pln, q, k, v, c, dc, lse, dq, dk, dv, sums):
        lane = lax.broadcasted_iota(jnp.int32, (1, pw), 1)
        sum_q = jnp.zeros((1, pw), F32)
        sum_v = jnp.zeros((1, pw), F32)
        for base, ln, which, i in sh.segs:
            n = (ql, pln)[which][i]
            rows = slice(base, base + ln)
            qb, kb, vb, dcb = q[rows, :], k[rows, :], v[rows, :], dc[rows, :]
            kt = kb.T
            prod = (dcb.astype(F32) * c[rows, :].astype(F32)).T
            keep = lax.broadcasted_iota(jnp.int32, (ln, 1), 0) < n
            dqs, dva, dka = [], None, None
            for h in range(2):
                mine = (lane >= h * hd) & (lane < (h + 1) * hd)
                zero = jnp.zeros_like(kb)
                kh = jnp.where(mine, kb, zero)
                qh = jnp.where(mine, qb, zero)
                dch = jnp.where(mine, dcb, zero)
                s = mm_nt(kh, qb) * (0.125 * LOG2E)
                s = jnp.where(keep, s, MASKED * LOG2E)
                p = jnp.exp2(s - lse[0, h : h + 1, rows])
                across = jnp.sum(prod[h * hd : (h + 1) * hd], axis=0, keepdims=True)
                ds = (p * (mm_nt(vb, dch) - across)).astype(BF)
                one_v = mm(p.astype(BF), dch)
                one_k = mm(ds, qh)
                dva = one_v if dva is None else dva + one_v
                dka = one_k if dka is None else dka + one_k
                dqs.append(mm(kt[h * hd : (h + 1) * hd], ds))
            dqa = jnp.concatenate(dqs, axis=0).T * 0.125
            dq[rows, :] = dqa.astype(BF)
            dk[rows, :] = (dka * 0.125).astype(BF)
            dv[rows, :] = dva.astype(BF)
            sum_q = sum_q + jnp.sum(dqa, axis=0, keepdims=True)
            sum_v = sum_v + jnp.sum(dva, axis=0, keepdims=True)
        sums[0:1, :] = sum_q
        sums[1:2, :] = sum_v

    def col(c):
        return pl.BlockSpec((sh.rows, pw), lambda j, *_: (0, c * pairs + j))

    grid_spec = pltpu.PrefetchScalarGridSpec(
        num_scalar_prefetch=2,
        grid=(pairs,),
        in_specs=[col(0), col(1), col(2), col(0), col(0)]
        + [pl.BlockSpec((1, 2, sh.rows), lambda j, *_: (j, 0, 0))],
        out_specs=[col(0)] * 3 + [pl.BlockSpec((2, pw), lambda j, *_: (0, j))],
    )
    sq = sum(ln * ln for _, ln, _, _ in sh.segs)
    return pl.pallas_call(
        body,
        grid_spec=grid_spec,
        out_shape=[sds((sh.rows, d), BF)] * 3 + [sds((2, d), F32)],
        compiler_params=params(32),
        cost_estimate=cost(4 * 10 * sq * d, sh.rows * d * 16, sq * HEADS),
    )(*lens, qkv, qkv, qkv, ctx, dctx, lse)


def first_norm(sh, ctx, xq, xp, w, small):
    d = ctx.shape[1]

    def body(c, xq, xp, w, sm, hat, scale, low):
        i = pl.program_id(0)
        x = jnp.where(i < sh.nq, xq[...], xp[...]).astype(F32)
        h = x + mm(c[...], w[...]) + sm[4:5, :]
        h = h - jnp.mean(h, axis=-1, keepdims=True)
        r = lax.rsqrt(jnp.mean(h * h, axis=-1, keepdims=True) + EPSILON)
        xhat = h * r
        hat[...] = xhat
        scale[...] = r
        low[...] = (xhat * sm[0:1, :] + sm[5:6, :]).astype(BF)

    return pl.pallas_call(
        body,
        grid=(sh.steps,),
        out_shape=[sds((sh.rows, d), F32), sds((sh.rows, 1), F32), sds((sh.rows, d), BF)],
        in_specs=[sh.rowspec(d)] + sh.both(d) + [VM, VM],
        out_specs=[sh.rowspec(d), sh.rowspec(1), sh.rowspec(d)],
        compiler_params=params(20),
        cost_estimate=cost(2 * sh.rows * d * d, sh.rows * d * 10),
    )(ctx, xq, xp, w, small)


def upward(sh, low, w, bias):
    d = low.shape[1]
    ff = w.shape[1]
    step = math.gcd(ff, 512)

    def body(low, w, b, act, slope):
        x = low[...]
        for c in range(0, ff, step):
            cols = slice(c, c + step)
            u = mm(x, w[:, cols]) + b[:, cols]
            t = 1.0 / (1.0 + TAIL_P * jnp.abs(u))
            poly = jnp.full_like(t, TAIL_C[-1])
            for co in TAIL_C[-2::-1]:
                poly = poly * t + co
            bell = jnp.exp2((u * u) * (-0.5 * LOG2E))
            tail = poly * t * bell
            phi = jnp.where(u > 0, 1.0 - tail, tail)
            act[:, cols] = (u * phi).astype(BF)
            slope[:, cols] = (phi + (u * (1.0 / math.sqrt(2.0 * math.pi))) * bell).astype(BF)

    return pl.pallas_call(
        body,
        grid=(sh.steps,),
        out_shape=[sds((sh.rows, ff), BF)] * 2,
        in_specs=[sh.rowspec(d), VM, VM],
        out_specs=[sh.rowspec(ff)] * 2,
        compiler_params=params(28),
        cost_estimate=cost(2 * sh.rows * d * ff, sh.rows * ff * 4, sh.rows * ff * 8),
    )(low, w, bias)


def second_norm(sh, lens, act, hat, cq, cp, w, small):
    d = hat.shape[1]
    ff = act.shape[1]

    def body(ql, pln, act, hat, cq, cp, w, sm, oq, op, dh, low, sums):
        i = pl.program_id(0)
        ok = sh.valid(i, (ql, pln))
        h = hat[...] * sm[0:1, :] + sm[5:6, :] + (mm(act[...], w[...]) + sm[6:7, :])
        h = h - jnp.mean(h, axis=-1, keepdims=True)
        r = lax.rsqrt(jnp.mean(h * h, axis=-1, keepdims=True) + EPSILON)
        xhat = h * r
        out = jnp.where(ok, xhat * sm[1:2, :] + sm[7:8, :], 0.0).astype(BF)

        @pl.when(i < sh.nq)
        def _():
            oq[...] = out

        @pl.when(i >= sh.nq)
        def _():
            op[...] = out

        dy = jnp.where(ok, jnp.where(i < sh.nq, cq[...], cp[...]).astype(F32), 0.0)
        t = dy * sm[1:2, :]
        prod = jnp.mean(t * xhat, axis=-1, keepdims=True)
        g = r * (t - jnp.mean(t, axis=-1, keepdims=True) - xhat * prod)
        dh[...] = g
        low[...] = g.astype(BF)
        rows = jnp.concatenate(
            [jnp.sum(z, axis=0, keepdims=True) for z in (dy * xhat, dy, g)], axis=0
        )

        @pl.when(i == 0)
        def _():
            sums[...] = rows

        @pl.when(i > 0)
        def _():
            sums[...] += rows

    grid_spec = pltpu.PrefetchScalarGridSpec(
        num_scalar_prefetch=2,
        grid=(sh.steps,),
        in_specs=[sh.rowspec(ff), sh.rowspec(d)] + sh.both(d) + [VM, VM],
        out_specs=sh.both(d) + [sh.rowspec(d), sh.rowspec(d), once((3, d))],
    )
    return pl.pallas_call(
        body,
        grid_spec=grid_spec,
        out_shape=[
            sds((sh.rq, d), BF),
            sds((sh.rp, d), BF),
            sds((sh.rows, d), F32),
            sds((sh.rows, d), BF),
            sds((3, d), F32),
        ],
        compiler_params=params(28),
        cost_estimate=cost(2 * sh.rows * d * ff, sh.rows * (ff * 2 + d * 14)),
    )(*lens, act, hat, cq, cp, w, small)


def up_back(sh, low, slope, w):
    d = low.shape[1]
    ff = w.shape[0]
    step = math.gcd(ff, 512)

    def body(low, slope, w, du, sums):
        i = pl.program_id(0)
        g = low[...]
        for c in range(0, ff, step):
            cols = slice(c, c + step)
            one = mm_nt(g, w[cols, :]) * slope[:, cols].astype(F32)
            du[:, cols] = one.astype(BF)
            row = jnp.sum(one, axis=0, keepdims=True)

            @pl.when(i == 0)
            def _():
                sums[:, cols] = row

            @pl.when(i > 0)
            def _():
                sums[:, cols] += row

    return pl.pallas_call(
        body,
        grid=(sh.steps,),
        out_shape=[sds((sh.rows, ff), BF), sds((1, ff), F32)],
        in_specs=[sh.rowspec(d), sh.rowspec(ff), VM],
        out_specs=[sh.rowspec(ff), once((1, ff))],
        compiler_params=params(24),
        cost_estimate=cost(2 * sh.rows * d * ff, sh.rows * ff * 4),
    )(low, slope, w)


def first_back(sh, du, dh2, hat, scale, wi, wo, small):
    d = hat.shape[1]
    ff = du.shape[1]

    def body(du, dh2, hat, r, wi, wo, sm, dh1, low, dctx, sums):
        i = pl.program_id(0)
        dn = dh2[...] + mm_nt(du[...], wi[...])
        xhat = hat[...]
        t = dn * sm[0:1, :]
        prod = jnp.mean(t * xhat, axis=-1, keepdims=True)
        g = r[...] * (t - jnp.mean(t, axis=-1, keepdims=True) - xhat * prod)
        glow = g.astype(BF)
        dh1[...] = g
        low[...] = glow
        dctx[...] = mm_nt(glow, wo[...]).astype(BF)
        rows = jnp.concatenate(
            [jnp.sum(z, axis=0, keepdims=True) for z in (dn * xhat, dn, g)], axis=0
        )

        @pl.when(i == 0)
        def _():
            sums[...] = rows

        @pl.when(i > 0)
        def _():
            sums[...] += rows

    return pl.pallas_call(
        body,
        grid=(sh.steps,),
        out_shape=[
            sds((sh.rows, d), F32),
            sds((sh.rows, d), BF),
            sds((sh.rows, d), BF),
            sds((3, d), F32),
        ],
        in_specs=[sh.rowspec(ff), sh.rowspec(d), sh.rowspec(d), sh.rowspec(1), VM, VM, VM],
        out_specs=[sh.rowspec(d)] * 3 + [once((3, d))],
        compiler_params=params(32),
        cost_estimate=cost(2 * sh.rows * d * (ff + d), sh.rows * (ff * 2 + d * 16)),
    )(du, dh2, hat, scale, wi, wo, small)


def weight_grad(lefts, rights):
    rows = [a.shape[0] for a in lefts]
    k = lefts[0].shape[1]
    widths = [b.shape[1] for b in rights]
    width = sum(widths)
    step = 256
    cut = 768
    total = sum(rows)

    def body(*refs):
        ls, rs, out = refs[: len(lefts)], refs[len(lefts) : -1], refs[-1]
        at = 0
        for b, w in zip(rs, widths):
            for c in range(0, w, cut):
                acc, base = None, 0
                for a, r in zip(ls, rows):
                    one = mm_tn(a[...], b[base : base + r, c : c + cut])
                    acc = one if acc is None else acc + one
                    base += r
                out[:, at + c : at + c + cut] = acc
            at += w

    return pl.pallas_call(
        body,
        grid=(k // step,),
        out_shape=sds((k, width), F32),
        in_specs=[pl.BlockSpec((r, step), lambda i: (0, i)) for r in rows] + [VM] * len(rights),
        out_specs=pl.BlockSpec((step, width), lambda i: (i, 0)),
        compiler_params=params(24),
        cost_estimate=cost(2 * total * k * width, total * (k + width) * 2 + k * width * 4),
    )(*lefts, *rights)


def input_grad(sh, dh1, parts, w):
    d = dh1.shape[1]

    def body(dh1, a, b, c, w, oq, op):
        i = pl.program_id(0)
        acc = dh1[...]
        for j, part in enumerate((a, b, c)):
            acc = acc + mm_nt(part[...], w[:, j * d : (j + 1) * d])
        out = acc.astype(BF)

        @pl.when(i < sh.nq)
        def _():
            oq[...] = out

        @pl.when(i >= sh.nq)
        def _():
            op[...] = out

    return pl.pallas_call(
        body,
        grid=(sh.steps,),
        out_shape=[sds((sh.rq, d), BF), sds((sh.rp, d), BF)],
        in_specs=[sh.rowspec(d)] * 4 + [VM],
        out_specs=sh.both(d),
        compiler_params=params(24),
        cost_estimate=cost(2 * sh.rows * d * 3 * d, sh.rows * d * 12),
    )(dh1, *parts, w)


def per_device(net, *args):
    xq3, xp3, ql, pln, cq3, cp3, w_qkv, w_out, w_inner, w_outer, gains, biases, inner_bias = args
    sh = Shape(xq3.shape[0], xq3.shape[1], xp3.shape[0], xp3.shape[1])
    lens = (ql, pln)
    d = xq3.shape[2]
    n = net.n
    own = d // n
    xq, xp = xq3.reshape(sh.rq, d), xp3.reshape(sh.rp, d)
    cq, cp = cq3.reshape(sh.rq, d), cp3.reshape(sh.rp, d)
    ff = inner_bias.shape[0] * n
    groups = ff // d
    custom = net.usable and own % 8 == 0 and ff // n <= 128 and own >= 9

    full_inner = lax.all_gather(w_inner, AXES, axis=0, tiled=True)
    if custom:
        tiny = jnp.zeros((own, 128), BF)
        tiny = lax.dynamic_update_slice(tiny, gains, (0, 0))
        tiny = lax.dynamic_update_slice(tiny, biases, (2, 0))
        tiny = lax.dynamic_update_slice(tiny, inner_bias[None], (8, 0))
        head = jnp.concatenate([w_qkv, tiny], axis=1)[None]
        pieces = net.gather_pieces(head)
        full_qkv, full_tiny = place(net, pieces, [(0, own, 1, 3 * d), (3 * d, own, 1, 128)])
        full_qkv = full_qkv.reshape(d, 3 * d)
        rest = jnp.concatenate(
            [w_out] + [w_outer[g * own : (g + 1) * own] for g in range(groups)], axis=1
        )[None]
        pieces = net.gather_pieces(rest)
        full_out, full_outer = place(net, pieces, [(0, own, 1, d), (d, own, groups, d)])
        full_out, full_outer = full_out.reshape(d, d), full_outer.reshape(ff, d)
        small = full_tiny[:, :8, :own].transpose(1, 0, 2).reshape(8, d).astype(F32)
        inner_shift = full_tiny[:, 8, : ff // n].reshape(1, ff).astype(F32)
    else:
        full_qkv = lax.all_gather(w_qkv, AXES, axis=0, tiled=True)
        full_out = lax.all_gather(w_out, AXES, axis=0, tiled=True)
        full_outer = lax.all_gather(w_outer, AXES, axis=0, tiled=True)
        small = lax.all_gather(jnp.concatenate([gains, biases], 0), AXES, axis=1, tiled=True).astype(F32)
        inner_shift = lax.all_gather(inner_bias, AXES, axis=0, tiled=True)[None].astype(F32)
    qkv_shift = jnp.concatenate([small[2:3], jnp.zeros((1, d), F32), small[3:4]], axis=1)

    qkv = qkv_project(sh, xq, xp, full_qkv, qkv_shift)
    ctx, lse = attend(sh, lens, qkv)
    hat1, scale1, low1 = first_norm(sh, ctx, xq, xp, full_out, small)
    act, slope = upward(sh, low1, full_inner, inner_shift)
    out_q, out_p, dh2, low2, sums2 = second_norm(sh, lens, act, hat1, cq, cp, full_outer, small)
    g_outer = weight_grad([act], [low2])
    du, sum_du = up_back(sh, low2, slope, full_outer)
    g_inner = weight_grad([low1], [du])
    dh1, low_a, dctx, sums1 = first_back(sh, du, dh2, hat1, scale1, full_inner, full_out, small)
    g_out = weight_grad([ctx], [low_a])
    dq, dk, dv, sums_qv = attend_back(sh, lens, qkv, ctx, dctx, lse)
    g_qkv = weight_grad([xq, xp], [dq, dk, dv])
    grad_q, grad_p = input_grad(sh, dh1, (dq, dk, dv), full_qkv)
    sums = jnp.concatenate(
        [sums1[0:1], sums2[0:1], sums_qv, sums1[2:3], sums1[1:2], sums2[2:3], sums2[1:2]], axis=0
    )
    if custom:
        r_outer = scatter_sum(net, g_outer.reshape(n, ff // n, d))
        r_inner = scatter_sum(net, g_inner.reshape(n, own, ff))
        r_out = scatter_sum(net, g_out.reshape(n, own, d))
        tiny = jnp.pad(sums.reshape(8, n, own).transpose(1, 0, 2), ((0, 0), (0, 0), (0, 128 - own)))
        tail = jnp.pad(sum_du.reshape(n, 1, ff // n), ((0, 0), (0, own - 9), (0, 128 - ff // n)))
        tiny = jnp.concatenate([tiny, tail], axis=1)
        both = jnp.concatenate([g_qkv.reshape(n, own, 3 * d), tiny], axis=2)
        r_both = scatter_sum(net, both)
        r_qkv, r_tiny = r_both[:, : 3 * d], r_both[:, 3 * d :]
        r_gains, r_biases, r_ib = r_tiny[:2, :own], r_tiny[2:8, :own], r_tiny[8, : ff // n]
    else:
        def rs(x, dim=0):
            return lax.psum_scatter(x, AXES, scatter_dimension=dim, tiled=True)

        r_outer, r_inner, r_out, r_qkv = rs(g_outer), rs(g_inner), rs(g_out), rs(g_qkv)
        r_sums = rs(sums, 1)
        r_gains, r_biases, r_ib = r_sums[:2], r_sums[2:], rs(sum_du[0])
    return (
        out_q.reshape(xq3.shape),
        out_p.reshape(xp3.shape),
        grad_q.reshape(xq3.shape),
        grad_p.reshape(xp3.shape),
        r_qkv,
        r_out,
        r_inner,
        r_outer,
        r_gains,
        r_biases,
        r_ib,
    )


def solution(mesh):
    rows3, rows2, row = P(AXES, None, None), P(AXES, None), P(AXES)
    cols = P(None, AXES)
    net = Net(mesh)
    return jax.shard_map(
        functools.partial(per_device, net),
        mesh=mesh,
        in_specs=(rows3, rows3, row, row, rows3, rows3, rows2, rows2, rows2, rows2, cols, cols, row),
        out_specs=(rows3, rows3, rows3, rows3, rows2, rows2, rows2, rows2, cols, cols, row),
        check_vma=False,
    )
```
